32 devices in a mesh: layer: 4 (over y, x), ex: 8 (over z, core).
Axes of the slice: x: 2, y: 2, z: 4, core: 2. Of those that a mesh axis runs over, the one named last changes fastest.
Arguments:
- query_factors: bfloat16 [4, 128, 512, 128], P('layer', 'ex'), may hold values from -1.2578125 to 1.2578125
- response_lengths: int32 [128], P('ex'), may hold values from 1 to 512, 32768 in all
- inverse_hessian: float32 [4, 4096, 4096], P('layer', 'ex'), as said below
- stored_gradients: bfloat16 [4, 2048, 4096], P('layer', 'ex'), may hold values from -0.015625 to 0.015625
Outputs:
- scores: float32 [128, 2048], P('layer', 'ex')
The draws below stay inside these ranges and needn't reach their ends.
Inputs may be any that keep to these rules, and one draw needn't show every extreme that they name: inverse_hessian[l] is symmetric for every layer l.
All inputs are finite; a program needn't handle non-finite values. No bound on the sum of `response_lengths` on one device may be relied on, other than what follows from the above.
Results may differ from the reference program's by a relative error of at most 0.004.
Values may be sent and summed in bfloat16 or wider, within the bound.
A program may use at most 64 MiB of HBM per device.

```python
import math
import jax
import jax.numpy as jnp
import numpy as np
from jax import lax

RANK = 64
DIM = 4096
MAXLEN = 512
LAYERS = 4
QUERIES = 128
EXAMPLES = 2048


def draw_inverse_hessian(key, part):
    first_key, second_key = jax.random.split(jax.random.fold_in(key, 17))
    noise = jax.random.normal(first_key, (LAYERS, DIM, DIM), jnp.float32)
    diagonal = jax.random.uniform(second_key, (LAYERS, DIM), jnp.float32, 2.5, 4.5)
    spread = 0.7
    symmetric = (noise + jnp.swapaxes(noise, 1, 2)) * (spread / math.sqrt(2.0 * DIM))
    return symmetric + diagonal[:, :, None] * jnp.eye(DIM, dtype=jnp.float32)[None, :, :]


def block_levels(rng, extent, cuts, least, high):
    level, own = 1.0, jax.random.fold_in(rng, 6)
    for position, parts in cuts:
        steps = jnp.exp(jax.random.uniform(jax.random.fold_in(own, position), (parts,), jnp.float32, least / len(cuts), high / len(cuts)))
        level = level * jnp.repeat(steps, extent[position] // parts).reshape([-1 if axis == position else 1 for axis in range(len(extent))])
    return level


def profile(amount, total, limit, slope):
    loads = [(1 << 20) // math.isqrt(grade ** slope) + 1 for grade in range(2, amount + 1)]
    rest, holding = total - limit - (amount - 1), [1] * (amount - 1)
    while rest > 0:
        movable = [i for i in range(amount - 1) if holding[i] < limit]
        whole, remaining = sum([loads[i] for i in movable]), rest
        for i in movable:
            extra = min(limit - holding[i], max(1, remaining * loads[i] // whole), rest)
            holding[i] = holding[i] + extra
            rest = rest - extra
    return np.array([limit] + holding)


def ragged(rng, count, total, most, skew):
    if count == 2:
        one = jax.random.randint(rng, (), max(1, total - most), min(most, total - 1) + 1)
        return jnp.stack([one, total - one])
    tallies = jnp.asarray(profile(count, total, most, skew), jnp.int32)
    couples = (count - 1) // 2
    giver, sink = tallies[1:1 + 2 * couples:2], tallies[2:2 + 2 * couples:2]
    room = jnp.minimum(giver - 1, most - sink)
    passed = jax.random.randint(jax.random.fold_in(rng, 1), (couples,), 0, 1 << 20) % (room + 1)
    tallies = tallies.at[1:1 + 2 * couples:2].set(giver - passed).at[2:2 + 2 * couples:2].set(sink + passed)
    return tallies[jax.random.permutation(jax.random.fold_in(rng, 2), count)]


def centred(stream_key, dims, width, most, shards=(), held_as=jnp.bfloat16):
    loudness = block_levels(stream_key, dims, shards, -0.22, 0.18) if shards else 1.0
    drawn = jax.random.normal(stream_key, dims, jnp.float32) * width * loudness
    return jnp.minimum(jnp.maximum(drawn, -most), most).astype(held_as)


def setup_inputs(seed: int = 0) -> dict:
    seeds = jax.random.split(jax.random.key(seed), 5)
    query_factors = centred(seeds[0], (LAYERS, QUERIES, MAXLEN, 2 * RANK), (MAXLEN ** -0.25), 1.2578125, ((0, 4), (1, 8)))
    response_lengths = ragged(seeds[1], QUERIES, QUERIES * MAXLEN // 2, MAXLEN, 2).astype(jnp.int32)
    inverse_hessian = draw_inverse_hessian(jax.random.fold_in(seeds[4], 71), 0)
    stored_gradients = centred(seeds[3], (LAYERS, EXAMPLES, DIM), (9 * DIM * LAYERS) ** -0.5, 0.015625, ((0, 4), (1, 8)))
    return dict(query_factors=query_factors, response_lengths=response_lengths, inverse_hessian=inverse_hessian, stored_gradients=stored_gradients)


def layer_scores(query_layer, response_lengths, inverse_layer, stored_layer):
    steps = jnp.arange(MAXLEN, dtype=jnp.int32)
    mask = (steps[None, :] < response_lengths[:, None]).astype(jnp.bfloat16)
    inputs = query_layer[:, :, :RANK] * mask[:, :, None]
    outputs = query_layer[:, :, RANK:]
    projected = jnp.einsum("qti,qtj->qij", outputs.astype(jnp.float32), inputs.astype(jnp.float32))
    projected = projected.reshape(QUERIES, DIM).astype(jnp.bfloat16)
    preconditioned = jnp.dot(projected.astype(jnp.float32), inverse_layer, precision=lax.Precision.HIGHEST, preferred_element_type=jnp.float32).astype(jnp.bfloat16)
    return lax.dot_general(preconditioned, stored_layer, (((1,), (1,)), ((), ())), preferred_element_type=jnp.float32)


def reference(query_factors, response_lengths, inverse_hessian, stored_gradients):
    def one_layer(carry, items):
        query_layer, inverse_layer, stored_layer = items
        return carry + layer_scores(query_layer, response_lengths, inverse_layer, stored_layer), None

    start = jnp.zeros((QUERIES, EXAMPLES), jnp.float32)
    scores, unused = lax.scan(one_layer, start, (query_factors, inverse_hessian, stored_gradients))
    return scores
```

```python
import functools

import jax
import jax.numpy as jnp
from jax import lax
from jax.experimental import pallas as pl
from jax.experimental.pallas import tpu as pltpu
from jax.sharding import PartitionSpec as P

MESH = pl.DeviceIdType.MESH
NT = (((1,), (1,)), ((), ()))


def form_gradients(query_layer, response_lengths):
    steps = lax.broadcasted_iota(jnp.int32, (query_layer.shape[0], query_layer.shape[1]), 1)
    mask = (steps < response_lengths[:, None]).astype(jnp.bfloat16)
    rank = query_layer.shape[2] // 2
    inputs = query_layer[:, :, :rank] * mask[:, :, None]
    outputs = query_layer[:, :, rank:]
    projected = jnp.einsum("qti,qtj->qij", outputs, inputs, preferred_element_type=jnp.float32)
    return projected.reshape(query_layer.shape[0], rank * rank).astype(jnp.bfloat16)


def per_device_plain(query_factors, response_lengths, inverse_hessian, stored_gradients):
    projected = form_gradients(query_factors[0], response_lengths)
    block_columns = lax.dot_general(
        lax.all_gather(projected, "ex", axis=0, tiled=True).astype(jnp.float32),
        inverse_hessian[0],
        NT,
        precision=lax.Precision.HIGHEST,
        preferred_element_type=jnp.float32,
    ).astype(jnp.bfloat16)
    layer_total = lax.dot_general(
        lax.all_gather(block_columns, "ex", axis=1, tiled=True),
        stored_gradients[0],
        NT,
        preferred_element_type=jnp.float32,
    )
    return lax.psum_scatter(layer_total, "layer", scatter_dimension=0, tiled=True)


class Line:
    def __init__(self, at, chips, chunks, send_sem, recv_sem):
        self.at, self.chips, self.chunks = at, chips, chunks
        self.send_sem, self.recv_sem = send_sem, recv_sem
        e = lax.axis_index("ex")
        self.z, self.c = e // 2, lax.rem(e, 2)

    def source(self, flow, o):
        z = self.z - o if flow == 0 else self.z + o
        return z * 2 + self.c

    def valid(self, flow, o):
        return self.z - o >= 0 if flow == 0 else self.z + o < self.chips

    def copy(self, block, k, send, recv, target):
        ref = self.at(block, k)
        return pltpu.make_async_remote_copy(
            src_ref=ref,
            dst_ref=ref,
            send_sem=self.send_sem.at[send + (k,)],
            recv_sem=self.recv_sem.at[recv + (k,)],
            device_id={"ex": target},
            device_id_type=MESH,
        )

    def onward(self, flow, o, k):
        step = 2 if flow == 0 else -2
        e = self.z * 2 + self.c
        return self.copy(self.source(flow, o), k, (flow, o), (flow, o + 1), e + step)

    def has_next(self, flow):
        return self.z < self.chips - 1 if flow == 0 else self.z > 0

    def aside(self, flow, o, k):
        partner = self.z * 2 + 1 - self.c
        return self.copy(self.source(flow, o), k, (2 + flow, o), (2 + flow, o), partner)

    def arrival(self, flow, o, k, other=False):
        e = self.z * 2 + self.c
        block = self.source(flow, o)
        if other:
            block = block + 1 - 2 * self.c
        row = (2 + flow, o) if other else (flow, o)
        return self.copy(block, k, (0, 0), row, e + 1 - 2 * self.c)

    def start_own(self, k):
        for flow in (0, 1):
            @pl.when(self.has_next(flow))
            def _():
                self.onward(flow, 0, k).start()
        self.aside(0, 0, k).start()

    def relay(self, flow, o, k):
        @pl.when(self.valid(flow, o))
        def _():
            self.arrival(flow, o, k).wait_recv()

            @pl.when(self.has_next(flow))
            def _():
                self.onward(flow, o, k).start()

            self.aside(flow, o, k).start()

    def wait_other(self, flow, o, k):
        self.arrival(flow, o, k, True).wait_recv()

    def finish(self):
        for k in range(self.chunks):
            self.aside(0, 0, k).wait_send()
            for flow in (0, 1):
                for o in range(self.chips):
                    if o:
                        @pl.when(self.valid(flow, o))
                        def _():
                            self.aside(flow, o, k).wait_send()
                    if o < self.chips - 1:
                        @pl.when(jnp.logical_and(self.valid(flow, o), self.has_next(flow)))
                        def _():
                            self.onward(flow, o, k).wait_send()


def kernel(
    chips, layers, ck, cm,
    lens, qf, hess, store, out,
    qv, hv, hhi, hlo, sv, gram, pall, pacc, preall, acc, landed,
    q_sem, h_sem, s_sem, send1, recv1, send2, recv2, send3, recv3,
):
    nq, steps, width = qv.shape
    rank = width // 2
    rows, depth = hv.shape[1], hv.shape[2]
    cores = 2 * chips
    l, e = lax.axis_index("layer"), lax.axis_index("ex")
    z, c = e // 2, lax.rem(e, 2)

    q_copy = pltpu.make_async_copy(qf.at[0], qv, q_sem)
    q_copy.start()
    h_copies = [
        pltpu.make_async_copy(hess.at[0, :, pl.ds(k * depth, depth)], hv.at[k], h_sem.at[k]) for k in range(ck)
    ]
    for copy in h_copies:
        copy.start()
    s_copies = [
        pltpu.make_async_copy(store.at[0, :, pl.ds(d * rows, rows)], sv.at[d], s_sem.at[d]) for d in range(cores)
    ]
    for copy in s_copies:
        copy.start()

    barrier = pltpu.get_barrier_semaphore()
    pl.semaphore_signal(barrier, inc=1, device_id={"ex": e + 1 - 2 * c}, device_id_type=MESH)
    for d in range(1, layers):
        pl.semaphore_signal(barrier, inc=1, device_id={"layer": lax.rem(l + d, layers)}, device_id_type=MESH)

    @pl.when(z > 0)
    def _():
        pl.semaphore_signal(barrier, inc=1, device_id={"ex": e - 2}, device_id_type=MESH)

    @pl.when(z < chips - 1)
    def _():
        pl.semaphore_signal(barrier, inc=1, device_id={"ex": e + 2}, device_id_type=MESH)

    q_copy.wait()
    token = lax.broadcasted_iota(jnp.int32, (steps, width), 0)

    def one_query(q, carry):
        x = qv[q]
        kept = jnp.where(token < lens[q], x.astype(jnp.float32), 0.0).astype(jnp.bfloat16)
        product = lax.dot_general(x, kept, (((0,), (0,)), ((), ())), preferred_element_type=jnp.float32)
        gram[pl.ds(pl.multiple_of(q * rank, rank), rank), :] = product[rank:, :]
        return carry

    lax.fori_loop(0, nq, one_query, 0, unroll=4)
    low = lax.broadcasted_iota(jnp.int32, (nq, width), 1) < rank
    for pair in range(rank // 2):
        even = gram[pl.ds(2 * pair, nq, stride=rank), :]
        odd = gram[pl.ds(2 * pair + 1, nq, stride=rank), :]
        both = jnp.where(low, even, pltpu.roll(odd, rank, 1))
        pall[e, :, pl.ds(pair * width, width)] = both.astype(jnp.bfloat16)

    neighbours = layers + (z > 0).astype(jnp.int32) + (z < chips - 1).astype(jnp.int32)
    pl.semaphore_wait(barrier, neighbours)

    first = Line(lambda b, k: pall.at[b, :, pl.ds(k * depth, depth)], chips, ck, send1, recv1)
    for k in range(ck):
        first.start_own(k)

    strip = 16

    def split(k):
        h_copies[k].wait()

        def body(i, carry):
            at = pl.ds(pl.multiple_of(i * strip, strip), strip)
            whole = hv[k, at, :]
            high = whole.astype(jnp.bfloat16)
            hhi[k, at, :] = high
            hlo[k, at, :] = (whole - high.astype(jnp.float32)).astype(jnp.bfloat16)
            return carry

        lax.fori_loop(0, rows // strip, body, 0)

    for k in range(ck):
        split(k)

    for o in range(1, chips):
        for k in range(ck):
            for flow in (0, 1):
                first.relay(flow, o, k)
            if o == chips - 1:
                first.wait_other(0, 0, k)
                for flow in (0, 1):
                    for p in range(1, chips):
                        @pl.when(first.valid(flow, p))
                        def _():
                            first.wait_other(flow, p, k)
                piece = pall[:, :, k * depth:(k + 1) * depth].reshape(cores * nq, depth)
                term = lax.dot_general(piece, hhi[k], NT, preferred_element_type=jnp.float32)
                term += lax.dot_general(piece, hlo[k], NT, preferred_element_type=jnp.float32)
                if k:
                    term += pacc[...]
                if k < ck - 1:
                    pacc[...] = term
                else:
                    preall[e] = term.astype(jnp.bfloat16)

    part = cores * nq // cm
    second = Line(lambda b, k: preall.at[b, pl.ds(k * part, part), :], chips, cm, send2, recv2)
    for k in range(cm):
        second.start_own(k)

    def scored(block):
        return lax.dot_general(preall[block], sv[block], NT, preferred_element_type=jnp.float32)

    for copy in s_copies:
        copy.wait()
    acc[...] = scored(e)
    for k in range(cm):
        second.wait_other(0, 0, k)
    acc[...] += scored(e + 1 - 2 * c)
    for o in range(1, chips):
        for k in range(cm):
            for flow in (0, 1):
                second.relay(flow, o, k)
        for flow in (0, 1):
            @pl.when(second.valid(flow, o))
            def _():
                acc[...] += scored(second.source(flow, o))
                for k in range(cm):
                    second.wait_other(flow, o, k)
                acc[...] += scored(second.source(flow, o) + 1 - 2 * c)

    share = cores * nq // layers
    copies = []
    for d in range(1, layers):
        target = lax.rem(l + d, layers)
        copy = pltpu.make_async_remote_copy(
            src_ref=acc.at[pl.ds(pl.multiple_of(target * share, share), share), :],
            dst_ref=landed.at[d - 1],
            send_sem=send3.at[d - 1],
            recv_sem=recv3.at[d - 1],
            device_id={"layer": target},
            device_id_type=MESH,
        )
        copy.start()
        copies.append(copy)
    total = acc[pl.ds(pl.multiple_of(l * share, share), share), :]
    for d in range(1, layers):
        copies[d - 1].wait_recv()
        total += landed[d - 1]
    out[...] = total
    for copy in copies:
        copy.wait_send()
    first.finish()
    second.finish()


def per_device(layers, cores, query_factors, response_lengths, inverse_hessian, stored_gradients):
    nq, steps, width = query_factors.shape[1:]
    rows, dim = inverse_hessian.shape[1:]
    examples = stored_gradients.shape[1]
    rank, chips, queries = width // 2, cores // 2, cores * nq
    ck, cm = 4, 4
    depth = dim // ck
    bf16, f32 = jnp.bfloat16, jnp.float32
    hbm = pl.BlockSpec(memory_space=pl.ANY)
    dma = pltpu.SemaphoreType.DMA
    return pl.pallas_call(
        functools.partial(kernel, chips, layers, ck, cm),
        out_shape=jax.ShapeDtypeStruct((queries // layers, examples), f32),
        in_specs=[pl.BlockSpec(memory_space=pltpu.SMEM), hbm, hbm, hbm],
        out_specs=pl.BlockSpec(memory_space=pltpu.VMEM),
        scratch_shapes=[
            pltpu.VMEM((nq, steps, width), bf16),
            pltpu.VMEM((ck, rows, depth), f32),
            pltpu.VMEM((ck, rows, depth), bf16),
            pltpu.VMEM((ck, rows, depth), bf16),
            pltpu.VMEM((cores, examples, rows), bf16),
            pltpu.VMEM((nq * rank, width), f32),
            pltpu.VMEM((cores, nq, dim), bf16),
            pltpu.VMEM((queries, rows), f32),
            pltpu.VMEM((cores, queries, rows), bf16),
            pltpu.VMEM((queries, examples), f32),
            pltpu.VMEM((layers - 1, queries // layers, examples), f32),
            dma,
            dma((ck,)),
            dma((cores,)),
            dma((4, chips, ck)),
            dma((4, chips, ck)),
            dma((4, chips, cm)),
            dma((4, chips, cm)),
            dma((layers - 1,)),
            dma((layers - 1,)),
        ],
        compiler_params=pltpu.CompilerParams(
            collective_id=0, has_side_effects=True, vmem_limit_bytes=56 * 1024 * 1024
        ),
    )(response_lengths, query_factors, inverse_hessian, stored_gradients)


def solution(mesh):
    layers, cores = mesh.shape["layer"], mesh.shape["ex"]
    placed = (P("layer", "ex", None, None), P("ex"), P("layer", "ex", None), P("layer", "ex", None))

    def body(query_factors, response_lengths, inverse_hessian, stored_gradients):
        args = (query_factors, response_lengths, inverse_hessian, stored_gradients)
        if cores % 2 or inverse_hessian.shape[1] % 128 or query_factors.shape[1] % 16:
            return per_device_plain(*args)
        return per_device(layers, cores, *args)

    return jax.shard_map(body, mesh=mesh, in_specs=placed, out_specs=P("layer", "ex"), check_vma=False)
```

```python
import functools

import jax
import jax.numpy as jnp
from jax import lax
from jax.experimental import pallas as pl
from jax.experimental.pallas import tpu as pltpu
from jax.sharding import PartitionSpec as P

MESH = pl.DeviceIdType.MESH
NT = (((1,), (1,)), ((), ()))


def form_gradients(query_layer, response_lengths):
    steps = lax.broadcasted_iota(jnp.int32, (query_layer.shape[0], query_layer.shape[1]), 1)
    mask = (steps < response_lengths[:, None]).astype(jnp.bfloat16)
    rank = query_layer.shape[2] // 2
    inputs = query_layer[:, :, :rank] * mask[:, :, None]
    outputs = query_layer[:, :, rank:]
    projected = jnp.einsum("qti,qtj->qij", outputs, inputs, preferred_element_type=jnp.float32)
    return projected.reshape(query_layer.shape[0], rank * rank).astype(jnp.bfloat16)


def per_device_plain(query_factors, response_lengths, inverse_hessian, stored_gradients):
    projected = form_gradients(query_factors[0], response_lengths)
    block_columns = lax.dot_general(
        lax.all_gather(projected, "ex", axis=0, tiled=True).astype(jnp.float32),
        inverse_hessian[0],
        NT,
        precision=lax.Precision.HIGHEST,
        preferred_element_type=jnp.float32,
    ).astype(jnp.bfloat16)
    layer_total = lax.dot_general(
        lax.all_gather(block_columns, "ex", axis=1, tiled=True),
        stored_gradients[0],
        NT,
        preferred_element_type=jnp.float32,
    )
    return lax.psum_scatter(layer_total, "layer", scatter_dimension=0, tiled=True)


class Line:
    def __init__(self, at, chips, chunks, send_sem, recv_sem):
        self.at, self.chips, self.chunks = at, chips, chunks
        self.send_sem, self.recv_sem = send_sem, recv_sem
        e = lax.axis_index("ex")
        self.z, self.c = e // 2, lax.rem(e, 2)

    def source(self, flow, o):
        z = self.z - o if flow == 0 else self.z + o
        return z * 2 + self.c

    def valid(self, flow, o):
        return self.z - o >= 0 if flow == 0 else self.z + o < self.chips

    def copy(self, block, k, send, recv, target):
        ref = self.at(block, k)
        return pltpu.make_async_remote_copy(
            src_ref=ref,
            dst_ref=ref,
            send_sem=self.send_sem.at[send + (k,)],
            recv_sem=self.recv_sem.at[recv + (k,)],
            device_id={"ex": target},
            device_id_type=MESH,
        )

    def onward(self, flow, o, k):
        step = 2 if flow == 0 else -2
        e = self.z * 2 + self.c
        return self.copy(self.source(flow, o), k, (flow, o), (flow, o + 1), e + step)

    def has_next(self, flow):
        return self.z < self.chips - 1 if flow == 0 else self.z > 0

    def aside(self, flow, o, k):
        partner = self.z * 2 + 1 - self.c
        return self.copy(self.source(flow, o), k, (2 + flow, o), (2 + flow, o), partner)

    def arrival(self, flow, o, k, other=False):
        e = self.z * 2 + self.c
        block = self.source(flow, o)
        if other:
            block = block + 1 - 2 * self.c
        row = (2 + flow, o) if other else (flow, o)
        return self.copy(block, k, (0, 0), row, e + 1 - 2 * self.c)

    def start_own(self, k):
        for flow in (0, 1):
            @pl.when(self.has_next(flow))
            def _():
                self.onward(flow, 0, k).start()
        self.aside(0, 0, k).start()

    def relay(self, flow, o, k):
        @pl.when(self.valid(flow, o))
        def _():
            self.arrival(flow, o, k).wait_recv()

            @pl.when(self.has_next(flow))
            def _():
                self.onward(flow, o, k).start()

            self.aside(flow, o, k).start()

    def wait_other(self, flow, o, k):
        self.arrival(flow, o, k, True).wait_recv()

    def finish(self):
        for k in range(self.chunks):
            self.aside(0, 0, k).wait_send()
            for flow in (0, 1):
                for o in range(self.chips):
                    if o:
                        @pl.when(self.valid(flow, o))
                        def _():
                            self.aside(flow, o, k).wait_send()
                    if o < self.chips - 1:
                        @pl.when(jnp.logical_and(self.valid(flow, o), self.has_next(flow)))
                        def _():
                            self.onward(flow, o, k).wait_send()


def kernel(
    chips, layers, ck, cm,
    lens, qf, hess, store, out,
    qv, hv, hhi, hlo, sv, gram, pall, pacc, preall, acc, landed,
    q_sem, h_sem, s_sem, send1, recv1, send2, recv2, send3, recv3,
):
    nq, steps, width = qv.shape
    rank = width // 2
    rows, depth = hv.shape[1], hv.shape[2]
    cores = 2 * chips
    l, e = lax.axis_index("layer"), lax.axis_index("ex")
    z, c = e // 2, lax.rem(e, 2)

    q_copy = pltpu.make_async_copy(qf.at[0], qv, q_sem)
    q_copy.start()
    h_copies = [
        pltpu.make_async_copy(hess.at[0, :, pl.ds(k * depth, depth)], hv.at[k], h_sem.at[k]) for k in range(ck)
    ]
    s_copies = [
        pltpu.make_async_copy(store.at[0, :, pl.ds(d * rows, rows)], sv.at[d], s_sem.at[d]) for d in range(cores)
    ]

    barrier = pltpu.get_barrier_semaphore()
    pl.semaphore_signal(barrier, inc=1, device_id={"ex": e + 1 - 2 * c}, device_id_type=MESH)
    for d in range(1, layers):
        pl.semaphore_signal(barrier, inc=1, device_id={"layer": lax.rem(l + d, layers)}, device_id_type=MESH)

    @pl.when(z > 0)
    def _():
        pl.semaphore_signal(barrier, inc=1, device_id={"ex": e - 2}, device_id_type=MESH)

    @pl.when(z < chips - 1)
    def _():
        pl.semaphore_signal(barrier, inc=1, device_id={"ex": e + 2}, device_id_type=MESH)

    q_copy.wait()
    for copy in h_copies + s_copies:
        copy.start()
    token = lax.broadcasted_iota(jnp.int32, (steps, width), 0)

    def one_query(q, carry):
        x = qv[q]
        kept = jnp.where(token < lens[q], x.astype(jnp.float32), 0.0).astype(jnp.bfloat16)
        product = lax.dot_general(x, kept, (((0,), (0,)), ((), ())), preferred_element_type=jnp.float32)
        gram[pl.ds(pl.multiple_of(q * rank, rank), rank), :] = product[rank:, :]
        return carry

    lax.fori_loop(0, nq, one_query, 0, unroll=4)
    low = lax.broadcasted_iota(jnp.int32, (nq, width), 1) < rank
    for pair in range(rank // 2):
        even = gram[pl.ds(2 * pair, nq, stride=rank), :]
        odd = gram[pl.ds(2 * pair + 1, nq, stride=rank), :]
        both = jnp.where(low, even, pltpu.roll(odd, rank, 1))
        pall[e, :, pl.ds(pair * width, width)] = both.astype(jnp.bfloat16)

    neighbours = layers + (z > 0).astype(jnp.int32) + (z < chips - 1).astype(jnp.int32)
    pl.semaphore_wait(barrier, neighbours)

    first = Line(lambda b, k: pall.at[b, :, pl.ds(k * depth, depth)], chips, ck, send1, recv1)
    for k in range(ck):
        first.start_own(k)

    strip = 16

    def split(k):
        h_copies[k].wait()

        def body(i, carry):
            at = pl.ds(pl.multiple_of(i * strip, strip), strip)
            whole = hv[k, at, :]
            high = whole.astype(jnp.bfloat16)
            hhi[k, at, :] = high
            hlo[k, at, :] = (whole - high.astype(jnp.float32)).astype(jnp.bfloat16)
            return carry

        lax.fori_loop(0, rows // strip, body, 0)

    for k in range(ck):
        split(k)

    def product(k):
        first.wait_other(0, 0, k)
        for flow in (0, 1):
            for p in range(1, chips):
                @pl.when(first.valid(flow, p))
                def _():
                    first.wait_other(flow, p, k)
        piece = pall[:, :, k * depth:(k + 1) * depth].reshape(cores * nq, depth)
        term = lax.dot_general(piece, hhi[k], NT, preferred_element_type=jnp.float32)
        term += lax.dot_general(piece, hlo[k], NT, preferred_element_type=jnp.float32)
        if k:
            term += pacc[...]
        if k < ck - 1:
            pacc[...] = term
        else:
            preall[e] = term.astype(jnp.bfloat16)

    farthest = jnp.maximum(z, chips - 1 - z)
    for o in range(1, chips):
        for k in range(ck):
            for flow in (0, 1):
                first.relay(flow, o, k)
            if 2 * o >= chips - 1 and k:
                @pl.when(farthest == o)
                def _():
                    product(k - 1)
        if 2 * o >= chips - 1:
            @pl.when(farthest == o)
            def _():
                product(ck - 1)

    part = cores * nq // cm
    second = Line(lambda b, k: preall.at[b, pl.ds(k * part, part), :], chips, cm, send2, recv2)
    for k in range(cm):
        second.start_own(k)

    def scored(block):
        return lax.dot_general(preall[block], sv[block], NT, preferred_element_type=jnp.float32)

    for copy in s_copies:
        copy.wait()
    def own_pair():
        acc[...] = scored(e)
        for k in range(cm):
            second.wait_other(0, 0, k)
        acc[...] += scored(e + 1 - 2 * c)

    def pair(flow, o):
        @pl.when(second.valid(flow, o))
        def _():
            for k in range(cm):
                second.wait_other(flow, o, k)
            acc[...] += scored(second.source(flow, o)) + scored(second.source(flow, o) + 1 - 2 * c)

    work = [own_pair]
    for o in range(1, chips):
        for k in range(cm):
            for flow in (0, 1):
                second.relay(flow, o, k)
            if k and work:
                work.pop(0)()
        for todo in work:
            todo()
        work = [functools.partial(pair, flow, o) for flow in (0, 1)]
    for todo in work:
        todo()

    share = cores * nq // layers
    copies = []
    for d in range(1, layers):
        target = lax.rem(l + d, layers)
        copy = pltpu.make_async_remote_copy(
            src_ref=acc.at[pl.ds(pl.multiple_of(target * share, share), share), :],
            dst_ref=landed.at[d - 1],
            send_sem=send3.at[d - 1],
            recv_sem=recv3.at[d - 1],
            device_id={"layer": target},
            device_id_type=MESH,
        )
        copy.start()
        copies.append(copy)
    total = acc[pl.ds(pl.multiple_of(l * share, share), share), :]
    for d in range(1, layers):
        copies[d - 1].wait_recv()
        total += landed[d - 1]
    out[...] = total
    for copy in copies:
        copy.wait_send()
    first.finish()
    second.finish()


def per_device(layers, cores, query_factors, response_lengths, inverse_hessian, stored_gradients):
    nq, steps, width = query_factors.shape[1:]
    rows, dim = inverse_hessian.shape[1:]
    examples = stored_gradients.shape[1]
    rank, chips, queries = width // 2, cores // 2, cores * nq
    ck, cm = 4, 4
    depth = dim // ck
    bf16, f32 = jnp.bfloat16, jnp.float32
    hbm = pl.BlockSpec(memory_space=pl.ANY)
    dma = pltpu.SemaphoreType.DMA
    return pl.pallas_call(
        functools.partial(kernel, chips, layers, ck, cm),
        out_shape=jax.ShapeDtypeStruct((queries // layers, examples), f32),
        in_specs=[pl.BlockSpec(memory_space=pltpu.SMEM), hbm, hbm, hbm],
        out_specs=pl.BlockSpec(memory_space=pltpu.VMEM),
        scratch_shapes=[
            pltpu.VMEM((nq, steps, width), bf16),
            pltpu.VMEM((ck, rows, depth), f32),
            pltpu.VMEM((ck, rows, depth), bf16),
            pltpu.VMEM((ck, rows, depth), bf16),
            pltpu.VMEM((cores, examples, rows), bf16),
            pltpu.VMEM((nq * rank, width), f32),
            pltpu.VMEM((cores, nq, dim), bf16),
            pltpu.VMEM((queries, rows), f32),
            pltpu.VMEM((cores, queries, rows), bf16),
            pltpu.VMEM((queries, examples), f32),
            pltpu.VMEM((layers - 1, queries // layers, examples), f32),
            dma,
            dma((ck,)),
            dma((cores,)),
            dma((4, chips, ck)),
            dma((4, chips, ck)),
            dma((4, chips, cm)),
            dma((4, chips, cm)),
            dma((layers - 1,)),
            dma((layers - 1,)),
        ],
        compiler_params=pltpu.CompilerParams(
            collective_id=0, has_side_effects=True, vmem_limit_bytes=56 * 1024 * 1024
        ),
    )(response_lengths, query_factors, inverse_hessian, stored_gradients)


def solution(mesh):
    layers, cores = mesh.shape["layer"], mesh.shape["ex"]
    placed = (P("layer", "ex", None, None), P("ex"), P("layer", "ex", None), P("layer", "ex", None))

    def body(query_factors, response_lengths, inverse_hessian, stored_gradients):
        args = (query_factors, response_lengths, inverse_hessian, stored_gradients)
        if cores % 2 or inverse_hessian.shape[1] % 128 or query_factors.shape[1] % 16:
            return per_device_plain(*args)
        return per_device(layers, cores, *args)

    return jax.shard_map(body, mesh=mesh, in_specs=placed, out_specs=P("layer", "ex"), check_vma=False)
```

```python
import functools

import jax
import jax.numpy as jnp
from jax import lax
from jax.experimental import pallas as pl
from jax.experimental.pallas import tpu as pltpu
from jax.sharding import PartitionSpec as P

MESH = pl.DeviceIdType.MESH
NT = (((1,), (1,)), ((), ()))


def form_gradients(query_layer, response_lengths):
    steps = lax.broadcasted_iota(jnp.int32, (query_layer.shape[0], query_layer.shape[1]), 1)
    mask = (steps < response_lengths[:, None]).astype(jnp.bfloat16)
    rank = query_layer.shape[2] // 2
    inputs = query_layer[:, :, :rank] * mask[:, :, None]
    outputs = query_layer[:, :, rank:]
    projected = jnp.einsum("qti,qtj->qij", outputs, inputs, preferred_element_type=jnp.float32)
    return projected.reshape(query_layer.shape[0], rank * rank).astype(jnp.bfloat16)


def per_device_plain(query_factors, response_lengths, inverse_hessian, stored_gradients):
    projected = form_gradients(query_factors[0], response_lengths)
    block_columns = lax.dot_general(
        lax.all_gather(projected, "ex", axis=0, tiled=True).astype(jnp.float32),
        inverse_hessian[0],
        NT,
        precision=lax.Precision.HIGHEST,
        preferred_element_type=jnp.float32,
    ).astype(jnp.bfloat16)
    layer_total = lax.dot_general(
        lax.all_gather(block_columns, "ex", axis=1, tiled=True),
        stored_gradients[0],
        NT,
        preferred_element_type=jnp.float32,
    )
    return lax.psum_scatter(layer_total, "layer", scatter_dimension=0, tiled=True)


class Line:
    def __init__(self, at, chips, chunks, send_sem, recv_sem):
        self.at, self.chips, self.chunks = at, chips, chunks
        self.send_sem, self.recv_sem = send_sem, recv_sem
        e = lax.axis_index("ex")
        self.z, self.c = e // 2, lax.rem(e, 2)

    def source(self, flow, o):
        z = self.z - o if flow == 0 else self.z + o
        return z * 2 + self.c

    def valid(self, flow, o):
        return self.z - o >= 0 if flow == 0 else self.z + o < self.chips

    def copy(self, block, k, send, recv, target):
        ref = self.at(block, k)
        return pltpu.make_async_remote_copy(
            src_ref=ref,
            dst_ref=ref,
            send_sem=self.send_sem.at[send + (k,)],
            recv_sem=self.recv_sem.at[recv + (k,)],
            device_id={"ex": target},
            device_id_type=MESH,
        )

    def onward(self, flow, o, k):
        step = 2 if flow == 0 else -2
        e = self.z * 2 + self.c
        return self.copy(self.source(flow, o), k, (flow, o), (flow, o + 1), e + step)

    def has_next(self, flow):
        return self.z < self.chips - 1 if flow == 0 else self.z > 0

    def aside(self, flow, o, k):
        partner = self.z * 2 + 1 - self.c
        return self.copy(self.source(flow, o), k, (2 + flow, o), (2 + flow, o), partner)

    def arrival(self, flow, o, k, other=False):
        e = self.z * 2 + self.c
        block = self.source(flow, o)
        if other:
            block = block + 1 - 2 * self.c
        row = (2 + flow, o) if other else (flow, o)
        return self.copy(block, k, (0, 0), row, e + 1 - 2 * self.c)

    def start_own(self, k):
        for flow in (0, 1):
            @pl.when(self.has_next(flow))
            def _():
                self.onward(flow, 0, k).start()
        self.aside(0, 0, k).start()

    def relay(self, flow, o, k):
        @pl.when(self.valid(flow, o))
        def _():
            self.arrival(flow, o, k).wait_recv()

            @pl.when(self.has_next(flow))
            def _():
                self.onward(flow, o, k).start()

            self.aside(flow, o, k).start()

    def wait_other(self, flow, o, k):
        self.arrival(flow, o, k, True).wait_recv()

    def finish(self):
        for k in range(self.chunks):
            self.aside(0, 0, k).wait_send()
            for flow in (0, 1):
                for o in range(self.chips):
                    if o:
                        @pl.when(self.valid(flow, o))
                        def _():
                            self.aside(flow, o, k).wait_send()
                    if o < self.chips - 1:
                        @pl.when(jnp.logical_and(self.valid(flow, o), self.has_next(flow)))
                        def _():
                            self.onward(flow, o, k).wait_send()


def kernel(
    chips, layers, ck,
    lens, qf, hess, store, out,
    qv, hv, hhi, hlo, sv, gram, pall, pacc, preall, acc, landed,
    q_sem, h_sem, s_sem, send1, recv1, send2, recv2, send3, recv3,
):
    nq, steps, width = qv.shape
    rank = width // 2
    rows, depth = hv.shape[1], hv.shape[2]
    cores = 2 * chips
    l, e = lax.axis_index("layer"), lax.axis_index("ex")
    z, c = e // 2, lax.rem(e, 2)

    q_copy = pltpu.make_async_copy(qf.at[0], qv, q_sem)
    q_copy.start()
    h_copies = [
        pltpu.make_async_copy(hess.at[0, :, pl.ds(k * depth, depth)], hv.at[k], h_sem.at[k]) for k in range(ck)
    ]
    s_copies = [
        pltpu.make_async_copy(store.at[0, :, pl.ds(d * rows, rows)], sv.at[d], s_sem.at[d]) for d in range(cores)
    ]

    barrier = pltpu.get_barrier_semaphore()
    pl.semaphore_signal(barrier, inc=1, device_id={"ex": e + 1 - 2 * c}, device_id_type=MESH)
    for d in range(1, layers):
        pl.semaphore_signal(barrier, inc=1, device_id={"layer": lax.rem(l + d, layers)}, device_id_type=MESH)

    @pl.when(z > 0)
    def _():
        pl.semaphore_signal(barrier, inc=1, device_id={"ex": e - 2}, device_id_type=MESH)

    @pl.when(z < chips - 1)
    def _():
        pl.semaphore_signal(barrier, inc=1, device_id={"ex": e + 2}, device_id_type=MESH)

    q_copy.wait()
    for copy in h_copies + s_copies:
        copy.start()
    token = lax.broadcasted_iota(jnp.int32, (steps, width), 0)

    def one_query(q, carry):
        x = qv[q]
        kept = jnp.where(token < lens[q], x.astype(jnp.float32), 0.0).astype(jnp.bfloat16)
        product = lax.dot_general(x, kept, (((0,), (0,)), ((), ())), preferred_element_type=jnp.float32)
        gram[pl.ds(pl.multiple_of(q * rank, rank), rank), :] = product[rank:, :]
        return carry

    lax.fori_loop(0, nq, one_query, 0, unroll=4)
    low = lax.broadcasted_iota(jnp.int32, (nq, width), 1) < rank
    for pair in range(rank // 2):
        even = gram[pl.ds(2 * pair, nq, stride=rank), :]
        odd = gram[pl.ds(2 * pair + 1, nq, stride=rank), :]
        both = jnp.where(low, even, pltpu.roll(odd, rank, 1))
        pall[e, :, pl.ds(pair * width, width)] = both.astype(jnp.bfloat16)

    neighbours = layers + (z > 0).astype(jnp.int32) + (z < chips - 1).astype(jnp.int32)
    pl.semaphore_wait(barrier, neighbours)

    first = Line(lambda b, k: pall.at[b, :, pl.ds(k * depth, depth)], chips, ck, send1, recv1)
    for k in range(ck):
        first.start_own(k)

    strip = 16

    def split(k):
        h_copies[k].wait()

        def body(i, carry):
            at = pl.ds(pl.multiple_of(i * strip, strip), strip)
            whole = hv[k, at, :]
            high = whole.astype(jnp.bfloat16)
            hhi[k, at, :] = high
            hlo[k, at, :] = (whole - high.astype(jnp.float32)).astype(jnp.bfloat16)
            return carry

        lax.fori_loop(0, rows // strip, body, 0)

    for k in range(ck):
        split(k)

    def product(k):
        first.wait_other(0, 0, k)
        for flow in (0, 1):
            for p in range(1, chips):
                @pl.when(first.valid(flow, p))
                def _():
                    first.wait_other(flow, p, k)
        piece = pall[:, :, k * depth:(k + 1) * depth].reshape(cores * nq, depth)
        term = lax.dot_general(piece, hhi[k], NT, preferred_element_type=jnp.float32)
        term += lax.dot_general(piece, hlo[k], NT, preferred_element_type=jnp.float32)
        if k:
            term += pacc[...]
        if k < ck - 1:
            pacc[...] = term
        else:
            preall[e] = term.astype(jnp.bfloat16)

    farthest = jnp.maximum(z, chips - 1 - z)
    for o in range(1, chips):
        for k in range(ck):
            for flow in (0, 1):
                first.relay(flow, o, k)
            if 2 * o >= chips - 1 and k:
                @pl.when(farthest == o)
                def _():
                    product(k - 1)
        if 2 * o >= chips - 1:
            @pl.when(farthest == o)
            def _():
                product(ck - 1)

    share = cores * nq // layers

    def rows_of(k):
        return pl.ds(pl.multiple_of(lax.rem(l + 1 + k, layers) * share, share), share)

    second = Line(lambda b, k: preall.at[b, rows_of(k), :], chips, layers, send2, recv2)
    for k in range(layers):
        second.start_own(k)

    def scored(block):
        return lax.dot_general(preall[block], sv[block], NT, preferred_element_type=jnp.float32)

    for copy in s_copies:
        copy.wait()
    def own_pair():
        acc[...] = scored(e)
        for k in range(layers):
            second.wait_other(0, 0, k)
        acc[...] += scored(e + 1 - 2 * c)

    def pair(flow, o):
        @pl.when(second.valid(flow, o))
        def _():
            for k in range(layers):
                second.wait_other(flow, o, k)
            acc[...] += scored(second.source(flow, o)) + scored(second.source(flow, o) + 1 - 2 * c)

    copies = [
        pltpu.make_async_remote_copy(
            src_ref=acc.at[rows_of(k), :],
            dst_ref=landed.at[k],
            send_sem=send3.at[k],
            recv_sem=recv3.at[k],
            device_id={"layer": lax.rem(l + 1 + k, layers)},
            device_id_type=MESH,
        )
        for k in range(layers - 1)
    ]

    def last_pairs(o, k):
        rows = rows_of(k)
        for flow in (0, 1):
            @pl.when(second.valid(flow, o))
            def _():
                block = second.source(flow, o)
                acc[rows, :] += lax.dot_general(
                    preall[block, rows, :], sv[block], NT, preferred_element_type=jnp.float32
                )
                second.wait_other(flow, o, k)
                block = block + 1 - 2 * c
                acc[rows, :] += lax.dot_general(
                    preall[block, rows, :], sv[block], NT, preferred_element_type=jnp.float32
                )
        if k < layers - 1:
            copies[k].start()

    def inner_pair(flow, o):
        @pl.when(farthest != o)
        def _():
            pair(flow, o)

    work = [own_pair]
    for o in range(1, chips):
        for k in range(layers):
            for flow in (0, 1):
                second.relay(flow, o, k)
            if work:
                work.pop(0)()
            if k:
                while work:
                    work.pop(0)()
                if 2 * o >= chips - 1:
                    @pl.when(farthest == o)
                    def _():
                        last_pairs(o, k - 1)
        while work:
            work.pop(0)()
        if 2 * o >= chips - 1:
            @pl.when(farthest == o)
            def _():
                last_pairs(o, layers - 1)
        if o < chips - 1:
            work = [functools.partial(inner_pair, flow, o) for flow in (0, 1)]

    total = acc[rows_of(layers - 1), :]
    for k in range(layers - 1):
        copies[k].wait_recv()
        total += landed[k]
    out[...] = total
    for copy in copies:
        copy.wait_send()
    first.finish()
    second.finish()


def per_device(layers, cores, query_factors, response_lengths, inverse_hessian, stored_gradients):
    nq, steps, width = query_factors.shape[1:]
    rows, dim = inverse_hessian.shape[1:]
    examples = stored_gradients.shape[1]
    rank, chips, queries = width // 2, cores // 2, cores * nq
    ck = 4
    depth = dim // ck
    bf16, f32 = jnp.bfloat16, jnp.float32
    hbm = pl.BlockSpec(memory_space=pl.ANY)
    dma = pltpu.SemaphoreType.DMA
    return pl.pallas_call(
        functools.partial(kernel, chips, layers, ck),
        out_shape=jax.ShapeDtypeStruct((queries // layers, examples), f32),
        in_specs=[pl.BlockSpec(memory_space=pltpu.SMEM), hbm, hbm, hbm],
        out_specs=pl.BlockSpec(memory_space=pltpu.VMEM),
        scratch_shapes=[
            pltpu.VMEM((nq, steps, width), bf16),
            pltpu.VMEM((ck, rows, depth), f32),
            pltpu.VMEM((ck, rows, depth), bf16),
            pltpu.VMEM((ck, rows, depth), bf16),
            pltpu.VMEM((cores, examples, rows), bf16),
            pltpu.VMEM((nq * rank, width), f32),
            pltpu.VMEM((cores, nq, dim), bf16),
            pltpu.VMEM((queries, rows), f32),
            pltpu.VMEM((cores, queries, rows), bf16),
            pltpu.VMEM((queries, examples), f32),
            pltpu.VMEM((layers - 1, queries // layers, examples), f32),
            dma,
            dma((ck,)),
            dma((cores,)),
            dma((4, chips, ck)),
            dma((4, chips, ck)),
            dma((4, chips, layers)),
            dma((4, chips, layers)),
            dma((layers - 1,)),
            dma((layers - 1,)),
        ],
        compiler_params=pltpu.CompilerParams(
            collective_id=0, has_side_effects=True, vmem_limit_bytes=56 * 1024 * 1024
        ),
    )(response_lengths, query_factors, inverse_hessian, stored_gradients)


def solution(mesh):
    layers, cores = mesh.shape["layer"], mesh.shape["ex"]
    placed = (P("layer", "ex", None, None), P("ex"), P("layer", "ex", None), P("layer", "ex", None))

    def body(query_factors, response_lengths, inverse_hessian, stored_gradients):
        args = (query_factors, response_lengths, inverse_hessian, stored_gradients)
        shares = query_factors.shape[1] * cores % (16 * layers)
        if cores % 2 or inverse_hessian.shape[1] % 128 or query_factors.shape[1] % 16 or shares:
            return per_device_plain(*args)
        return per_device(layers, cores, *args)

    return jax.shard_map(body, mesh=mesh, in_specs=placed, out_specs=P("layer", "ex"), check_vma=False)
```

```python
import functools

import jax
import jax.numpy as jnp
from jax import lax
from jax.experimental import pallas as pl
from jax.experimental.pallas import tpu as pltpu
from jax.sharding import PartitionSpec as P

MESH = pl.DeviceIdType.MESH
NT = (((1,), (1,)), ((), ()))


def form_gradients(query_layer, response_lengths):
    steps = lax.broadcasted_iota(jnp.int32, (query_layer.shape[0], query_layer.shape[1]), 1)
    mask = (steps < response_lengths[:, None]).astype(jnp.bfloat16)
    rank = query_layer.shape[2] // 2
    inputs = query_layer[:, :, :rank] * mask[:, :, None]
    outputs = query_layer[:, :, rank:]
    projected = jnp.einsum("qti,qtj->qij", outputs, inputs, preferred_element_type=jnp.float32)
    return projected.reshape(query_layer.shape[0], rank * rank).astype(jnp.bfloat16)


def per_device_plain(query_factors, response_lengths, inverse_hessian, stored_gradients):
    projected = form_gradients(query_factors[0], response_lengths)
    block_columns = lax.dot_general(
        lax.all_gather(projected, "ex", axis=0, tiled=True).astype(jnp.float32),
        inverse_hessian[0],
        NT,
        precision=lax.Precision.HIGHEST,
        preferred_element_type=jnp.float32,
    ).astype(jnp.bfloat16)
    layer_total = lax.dot_general(
        lax.all_gather(block_columns, "ex", axis=1, tiled=True),
        stored_gradients[0],
        NT,
        preferred_element_type=jnp.float32,
    )
    return lax.psum_scatter(layer_total, "layer", scatter_dimension=0, tiled=True)


class Line:
    def __init__(self, at, chips, chunks, send_sem, recv_sem):
        self.at, self.chips, self.chunks = at, chips, chunks
        self.send_sem, self.recv_sem = send_sem, recv_sem
        e = lax.axis_index("ex")
        self.z, self.c = e // 2, lax.rem(e, 2)

    def source(self, flow, o):
        z = self.z - o if flow == 0 else self.z + o
        return z * 2 + self.c

    def valid(self, flow, o):
        return self.z - o >= 0 if flow == 0 else self.z + o < self.chips

    def copy(self, block, k, send, recv, target):
        ref = self.at(block, k)
        return pltpu.make_async_remote_copy(
            src_ref=ref,
            dst_ref=ref,
            send_sem=self.send_sem.at[send + (k,)],
            recv_sem=self.recv_sem.at[recv + (k,)],
            device_id={"ex": target},
            device_id_type=MESH,
        )

    def onward(self, flow, o, k):
        step = 2 if flow == 0 else -2
        e = self.z * 2 + self.c
        return self.copy(self.source(flow, o), k, (flow, o), (flow, o + 1), e + step)

    def has_next(self, flow):
        return self.z < self.chips - 1 if flow == 0 else self.z > 0

    def aside(self, flow, o, k):
        partner = self.z * 2 + 1 - self.c
        return self.copy(self.source(flow, o), k, (2 + flow, o), (2 + flow, o), partner)

    def arrival(self, flow, o, k, other=False):
        e = self.z * 2 + self.c
        block = self.source(flow, o)
        if other:
            block = block + 1 - 2 * self.c
        row = (2 + flow, o) if other else (flow, o)
        return self.copy(block, k, (0, 0), row, e + 1 - 2 * self.c)

    def start_own(self, k):
        for flow in (0, 1):
            @pl.when(self.has_next(flow))
            def _():
                self.onward(flow, 0, k).start()
        self.aside(0, 0, k).start()

    def relay(self, flow, o, k):
        @pl.when(self.valid(flow, o))
        def _():
            self.arrival(flow, o, k).wait_recv()

            @pl.when(self.has_next(flow))
            def _():
                self.onward(flow, o, k).start()

            self.aside(flow, o, k).start()

    def wait_other(self, flow, o, k):
        self.arrival(flow, o, k, True).wait_recv()

    def finish(self):
        for k in range(self.chunks):
            self.aside(0, 0, k).wait_send()
            for flow in (0, 1):
                for o in range(self.chips):
                    if o:
                        @pl.when(self.valid(flow, o))
                        def _():
                            self.aside(flow, o, k).wait_send()
                    if o < self.chips - 1:
                        @pl.when(jnp.logical_and(self.valid(flow, o), self.has_next(flow)))
                        def _():
                            self.onward(flow, o, k).wait_send()


def kernel(
    chips, layers, ck,
    lens, qf, hess, store, out,
    qv, hv, hhi, hlo, sv, gram, pall, pacc, preall, acc, landed,
    q_sem, h_sem, s_sem, send1, recv1, send2, recv2, send3, recv3,
):
    nq, steps, width = qv.shape
    rank = width // 2
    rows, depth = hv.shape[1], hv.shape[2]
    cores = 2 * chips
    l, e = lax.axis_index("layer"), lax.axis_index("ex")
    z, c = e // 2, lax.rem(e, 2)

    q_copy = pltpu.make_async_copy(qf.at[0], qv, q_sem)
    q_copy.start()
    h_copies = [
        pltpu.make_async_copy(hess.at[0, :, pl.ds(k * depth, depth)], hv.at[k], h_sem.at[k]) for k in range(ck)
    ]
    s_copies = [
        pltpu.make_async_copy(store.at[0, :, pl.ds(d * rows, rows)], sv.at[d], s_sem.at[d]) for d in range(cores)
    ]

    barrier = pltpu.get_barrier_semaphore()
    pl.semaphore_signal(barrier, inc=1, device_id={"ex": e + 1 - 2 * c}, device_id_type=MESH)
    for d in range(1, layers):
        pl.semaphore_signal(barrier, inc=1, device_id={"layer": lax.rem(l + d, layers)}, device_id_type=MESH)

    @pl.when(z > 0)
    def _():
        pl.semaphore_signal(barrier, inc=1, device_id={"ex": e - 2}, device_id_type=MESH)

    @pl.when(z < chips - 1)
    def _():
        pl.semaphore_signal(barrier, inc=1, device_id={"ex": e + 2}, device_id_type=MESH)

    q_copy.wait()
    for copy in h_copies + s_copies:
        copy.start()
    token = lax.broadcasted_iota(jnp.int32, (steps, width), 0)

    def one_query(q, carry):
        x = qv[q]
        kept = jnp.where(token < lens[q], x.astype(jnp.float32), 0.0).astype(jnp.bfloat16)
        product = lax.dot_general(x, kept, (((0,), (0,)), ((), ())), preferred_element_type=jnp.float32)
        gram[pl.ds(pl.multiple_of(q * rank, rank), rank), :] = product[rank:, :]
        return carry

    lax.fori_loop(0, nq, one_query, 0, unroll=4)
    low = lax.broadcasted_iota(jnp.int32, (nq, width), 1) < rank
    for pair in range(rank // 2):
        even = gram[pl.ds(2 * pair, nq, stride=rank), :]
        odd = gram[pl.ds(2 * pair + 1, nq, stride=rank), :]
        both = jnp.where(low, even, pltpu.roll(odd, rank, 1))
        pall[e, :, pl.ds(pair * width, width)] = both.astype(jnp.bfloat16)

    neighbours = layers + (z > 0).astype(jnp.int32) + (z < chips - 1).astype(jnp.int32)
    pl.semaphore_wait(barrier, neighbours)

    first = Line(lambda b, k: pall.at[b, :, pl.ds(k * depth, depth)], chips, ck, send1, recv1)
    for k in range(ck):
        first.start_own(k)

    strip = 16

    def split(k):
        h_copies[k].wait()

        def body(i, carry):
            at = pl.ds(pl.multiple_of(i * strip, strip), strip)
            whole = hv[k, at, :]
            high = whole.astype(jnp.bfloat16)
            hhi[k, at, :] = high
            hlo[k, at, :] = (whole - high.astype(jnp.float32)).astype(jnp.bfloat16)
            return carry

        lax.fori_loop(0, rows // strip, body, 0)

    def product(k):
        first.wait_other(0, 0, k)
        for flow in (0, 1):
            for p in range(1, chips):
                @pl.when(first.valid(flow, p))
                def _():
                    first.wait_other(flow, p, k)
        piece = pall[:, :, k * depth:(k + 1) * depth].reshape(cores * nq, depth)
        term = lax.dot_general(piece, hhi[k], NT, preferred_element_type=jnp.float32)
        term += lax.dot_general(piece, hlo[k], NT, preferred_element_type=jnp.float32)
        if k:
            term += pacc[...]
        if k < ck - 1:
            pacc[...] = term
        else:
            preall[e] = term.astype(jnp.bfloat16)

    farthest = jnp.maximum(z, chips - 1 - z)
    for o in range(1, chips):
        for k in range(ck):
            for flow in (0, 1):
                first.relay(flow, o, k)
            if o == 1:
                split(k)
            if 2 * o >= chips - 1 and k:
                @pl.when(farthest == o)
                def _():
                    product(k - 1)
        if 2 * o >= chips - 1:
            @pl.when(farthest == o)
            def _():
                product(ck - 1)

    share = cores * nq // layers

    def rows_of(k):
        return pl.ds(pl.multiple_of(lax.rem(l + 1 + k, layers) * share, share), share)

    second = Line(lambda b, k: preall.at[b, rows_of(k), :], chips, layers, send2, recv2)
    for k in range(layers):
        second.start_own(k)

    def scored(block):
        return lax.dot_general(preall[block], sv[block], NT, preferred_element_type=jnp.float32)

    for copy in s_copies:
        copy.wait()
    def own_pair():
        acc[...] = scored(e)
        for k in range(layers):
            second.wait_other(0, 0, k)
        acc[...] += scored(e + 1 - 2 * c)

    def pair(flow, o):
        @pl.when(second.valid(flow, o))
        def _():
            for k in range(layers):
                second.wait_other(flow, o, k)
            acc[...] += scored(second.source(flow, o)) + scored(second.source(flow, o) + 1 - 2 * c)

    copies = [
        pltpu.make_async_remote_copy(
            src_ref=acc.at[rows_of(k), :],
            dst_ref=landed.at[k],
            send_sem=send3.at[k],
            recv_sem=recv3.at[k],
            device_id={"layer": lax.rem(l + 1 + k, layers)},
            device_id_type=MESH,
        )
        for k in range(layers - 1)
    ]

    def last_pairs(o, k):
        rows = rows_of(k)
        for flow in (0, 1):
            @pl.when(second.valid(flow, o))
            def _():
                block = second.source(flow, o)
                acc[rows, :] += lax.dot_general(
                    preall[block, rows, :], sv[block], NT, preferred_element_type=jnp.float32
                )
                second.wait_other(flow, o, k)
                block = block + 1 - 2 * c
                acc[rows, :] += lax.dot_general(
                    preall[block, rows, :], sv[block], NT, preferred_element_type=jnp.float32
                )
        if k < layers - 1:
            copies[k].start()

    def inner_pair(flow, o):
        @pl.when(farthest != o)
        def _():
            pair(flow, o)

    work = [own_pair]
    for o in range(1, chips):
        for k in range(layers):
            for flow in (0, 1):
                second.relay(flow, o, k)
            if work:
                work.pop(0)()
            if k:
                while work:
                    work.pop(0)()
                if 2 * o >= chips - 1:
                    @pl.when(farthest == o)
                    def _():
                        last_pairs(o, k - 1)
        while work:
            work.pop(0)()
        if 2 * o >= chips - 1:
            @pl.when(farthest == o)
            def _():
                last_pairs(o, layers - 1)
        if o < chips - 1:
            work = [functools.partial(inner_pair, flow, o) for flow in (0, 1)]

    total = acc[rows_of(layers - 1), :]
    for k in range(layers - 1):
        copies[k].wait_recv()
        total += landed[k]
    out[...] = total
    for copy in copies:
        copy.wait_send()
    first.finish()
    second.finish()


def per_device(layers, cores, query_factors, response_lengths, inverse_hessian, stored_gradients):
    nq, steps, width = query_factors.shape[1:]
    rows, dim = inverse_hessian.shape[1:]
    examples = stored_gradients.shape[1]
    rank, chips, queries = width // 2, cores // 2, cores * nq
    ck = 4
    depth = dim // ck
    bf16, f32 = jnp.bfloat16, jnp.float32
    hbm = pl.BlockSpec(memory_space=pl.ANY)
    dma = pltpu.SemaphoreType.DMA
    return pl.pallas_call(
        functools.partial(kernel, chips, layers, ck),
        out_shape=jax.ShapeDtypeStruct((queries // layers, examples), f32),
        in_specs=[pl.BlockSpec(memory_space=pltpu.SMEM), hbm, hbm, hbm],
        out_specs=pl.BlockSpec(memory_space=pltpu.VMEM),
        scratch_shapes=[
            pltpu.VMEM((nq, steps, width), bf16),
            pltpu.VMEM((ck, rows, depth), f32),
            pltpu.VMEM((ck, rows, depth), bf16),
            pltpu.VMEM((ck, rows, depth), bf16),
            pltpu.VMEM((cores, examples, rows), bf16),
            pltpu.VMEM((nq * rank, width), f32),
            pltpu.VMEM((cores, nq, dim), bf16),
            pltpu.VMEM((queries, rows), f32),
            pltpu.VMEM((cores, queries, rows), bf16),
            pltpu.VMEM((queries, examples), f32),
            pltpu.VMEM((layers - 1, queries // layers, examples), f32),
            dma,
            dma((ck,)),
            dma((cores,)),
            dma((4, chips, ck)),
            dma((4, chips, ck)),
            dma((4, chips, layers)),
            dma((4, chips, layers)),
            dma((layers - 1,)),
            dma((layers - 1,)),
        ],
        compiler_params=pltpu.CompilerParams(
            collective_id=0, has_side_effects=True, vmem_limit_bytes=56 * 1024 * 1024
        ),
    )(response_lengths, query_factors, inverse_hessian, stored_gradients)


def solution(mesh):
    layers, cores = mesh.shape["layer"], mesh.shape["ex"]
    placed = (P("layer", "ex", None, None), P("ex"), P("layer", "ex", None), P("layer", "ex", None))

    def body(query_factors, response_lengths, inverse_hessian, stored_gradients):
        args = (query_factors, response_lengths, inverse_hessian, stored_gradients)
        shares = query_factors.shape[1] * cores % (16 * layers)
        if cores < 4 or cores % 2 or inverse_hessian.shape[1] % 128 or query_factors.shape[1] % 16 or shares:
            return per_device_plain(*args)
        return per_device(layers, cores, *args)

    return jax.shard_map(body, mesh=mesh, in_specs=placed, out_specs=P("layer", "ex"), check_vma=False)
```
